32 devices in a mesh: expert: 16 (over z, y, core), token: 2 (over x).
Axes of the slice: x: 2, y: 2, z: 4, core: 2. Of those that a mesh axis runs over, the one named last changes fastest.
Arguments:
- tokens: bfloat16 [512, 2048], P(('expert', 'token')), may hold values from -6 to 6
- routes: int32 [512, 8], P(('expert', 'token')), may hold values from 0 to 15, all different within a row; in each aligned block of 16 rows (0 to 15, 16 to 31, ...) at most 16 rows name the same one
- assign: int32 [16], replicated, may hold values from 0 to 3, as said below
- gate_weight: bfloat16 [16, 2048, 1536], P('expert', None, 'token'), may hold values from -0.125 to 0.125
- up_weight: bfloat16 [16, 2048, 1536], P('expert', None, 'token'), may hold values from -0.125 to 0.125
- sketch: bfloat16 [16, 1536, 512], P('expert', 'token'), may hold values from -6 to 6
Outputs:
- hidden: bfloat16 [16, 512, 1536], P('expert', None, 'token')
The draws below stay inside these ranges and needn't reach their ends.
Inputs may be any that keep to these rules, and one draw needn't show every extreme that they name: `routes`: within each aligned block of 16 tokens each token names 8 different experts, and no expert is named by more than 16 entries of the block. `assign`: every one of the 4 clusters has at least two experts.
All inputs are finite; a program needn't handle non-finite values.
Results may differ from the reference program's by a relative error of at most 0.029.
Values may be sent and summed in bfloat16 or wider, within the bound.
No kernel may reach another device: no remote copies, remote signals or barrier semaphores. Data moves between devices by JAX's collectives and lax.ppermute only.
A program may use at most 64 MiB of HBM per device.

```python
import math
import jax
import jax.numpy as jnp
import numpy as np
from jax import lax

D = 2048
FF = 1536
R = 512
TOP = 8
ITERS = 1
TOK_DEV = 16
EXPERTS = 16
CLUSTERS = 4
CAP = 16
SLOTS = 512
TOKENS = 512
N_TOKEN = 2


def draw_assign(key, part):
    cluster_count = CLUSTERS
    extra_total = EXPERTS - 2 * cluster_count
    head_extra = min(6, extra_total)
    rest_extra = extra_total - head_extra
    base_key = jax.random.fold_in(key, 11)
    key_slots = jax.random.fold_in(base_key, 1)
    key_labels = jax.random.fold_in(base_key, 2)
    key_experts = jax.random.fold_in(base_key, 3)
    slot_order = jax.random.permutation(key_slots, 6 * (cluster_count - 1))
    chosen = (slot_order < rest_extra).astype(jnp.int32).reshape(cluster_count - 1, 6).sum(axis=1)
    cluster_sizes = jnp.concatenate([jnp.full((1,), 2 + head_extra, jnp.int32), 2 + chosen])
    bounds = jnp.cumsum(cluster_sizes)
    position = jnp.arange(EXPERTS, dtype=jnp.int32)
    cluster_of = jnp.sum((position[:, None] >= bounds[None, :]).astype(jnp.int32), axis=1)
    labels = jax.random.permutation(key_labels, cluster_count).astype(jnp.int32)
    expert_order = jax.random.permutation(key_experts, EXPERTS)
    return jnp.zeros((EXPERTS,), jnp.int32).at[expert_order].set(labels[cluster_of])


def level_of(own_key, extent, shards, smallest, top_value):
    gain, own = 1.0, jax.random.fold_in(own_key, 6)
    for dim, shards_of in shards:
        draws = jnp.exp(jax.random.uniform(jax.random.fold_in(own, dim), (shards_of,), jnp.float32, smallest / len(shards), top_value / len(shards)))
        gain = gain * jnp.repeat(draws, extent[dim] // shards_of).reshape([-1 if axis == dim else 1 for axis in range(len(extent))])
    return gain


def assign_block(stream_key, own, number, rows, number_of, top, bound, skew):
    order = jax.random.permutation(stream_key, number_of)
    heavy_load, usual = load_shares(number_of, rows * top, bound, skew, True), load_shares(number_of, rows * top, bound, skew, False)
    places = jnp.arange(number_of)

    def named(tallies, offset_by):
        used = int((tallies > 0).sum())
        fixed = max(1, used // 4)
        moved = fixed + (places - fixed + offset_by * (used - fixed)) % max(1, number_of - fixed)
        return jnp.zeros((number_of,), jnp.int32).at[order[jnp.where(places < fixed, places, moved)]].set(jnp.asarray(tallies, jnp.int32))

    tallies = jnp.where(number % 4 == 0, named(heavy_load, number // 4), named(usual, number - number // 4 - 1))
    mixed = jax.random.permutation(jax.random.fold_in(own, 3), number_of)
    giver, sink = mixed[0:number_of // 2 * 2:2], mixed[1:number_of // 2 * 2:2]
    margin = jnp.minimum(tallies[giver] - 1, bound - tallies[sink]) // 2
    margin = jnp.where((giver == order[0]) | (sink == order[0]) | (tallies[sink] == 0), 0, jnp.maximum(margin, 0))
    moved = jax.random.randint(jax.random.fold_in(own, 4), (number_of // 2,), 0, 1 << 20) % (margin + 1)
    tallies = tallies.at[giver].add(-moved).at[sink].add(moved)
    members = jnp.searchsorted(jnp.cumsum(tallies), jnp.arange(rows * top), side="right").astype(jnp.int32)
    listing = members.reshape(top, rows).T
    listing = listing[jax.random.permutation(jax.random.fold_in(own, 1), rows)]
    offset_by = jax.random.randint(jax.random.fold_in(own, 2), (rows, 1), 0, top)
    return jnp.take_along_axis(listing, (jnp.arange(top)[None, :] + offset_by) % top, axis=1)


def load_shares(count, total, reach, lean, full):
    portions = [(1 << 20) // math.isqrt(rank ** lean) + 1 for rank in range(1, count + 1)]
    largest = reach if full else min(reach, max(-(-total // count), total * portions[0] // sum(portions)))
    least = 1 if total - largest >= count - 1 else 0
    given, surplus = [largest] + [least] * (count - 1), total - largest - least * (count - 1)
    while surplus > 0:
        free = [i for i in range(1, count) if given[i] < largest] or [i for i in range(1, count) if given[i] < reach]
        mass, left = sum([portions[i] for i in free]), surplus
        for i in free:
            addition = min(reach - given[i], max(1, left * portions[i] // mass), surplus)
            given[i] = given[i] + addition
            surplus = surplus - addition
    return np.array(given)


def noise(key, extent, spread, most, split=(), kind=jnp.bfloat16):
    drawn = spread * jax.random.normal(key, extent, jnp.float32)
    if split:
        drawn = drawn * level_of(key, extent, split, -0.22, 0.18)
    return jnp.clip(drawn, -most, most).astype(kind)


def setup_inputs(seed: int = 0) -> dict:
    arg_keys = jax.random.split(jax.random.key(seed), 7)
    tokens = noise(arg_keys[0], (TOKENS, D), 1.0, 6.0, ((0, 32),))
    routes_keys = jax.random.split(jax.random.fold_in(arg_keys[1], 1), TOKENS // TOK_DEV)
    routes_turns = jax.random.permutation(jax.random.fold_in(arg_keys[1], 3), TOKENS // TOK_DEV)
    routes = jax.vmap(lambda own, number: assign_block(jax.random.fold_in(arg_keys[1], 2), own, number, TOK_DEV, EXPERTS, TOP, CAP, 2))(routes_keys, routes_turns).reshape((TOKENS, TOP))
    assign = draw_assign(jax.random.fold_in(arg_keys[6], 71), 0)
    gate_weight = noise(arg_keys[3], (EXPERTS, D, FF), D ** -0.5, 0.125, ((0, 16), (2, 2)))
    up_weight = noise(arg_keys[4], (EXPERTS, D, FF), D ** -0.5, 0.125, ((0, 16), (2, 2)))
    sketch = noise(arg_keys[5], (EXPERTS, FF, R), 1.0, 6.0, ((0, 16), (1, 2)))
    return dict(tokens=tokens, routes=routes, assign=assign, gate_weight=gate_weight, up_weight=up_weight, sketch=sketch)


def orthonormal(cluster_sum):
    rounded = lax.optimization_barrier(cluster_sum.astype(jnp.bfloat16)).astype(jnp.float32)
    column_gram = jnp.dot(rounded.T, rounded, precision=lax.Precision.HIGHEST)
    lower_factor = jnp.linalg.cholesky(column_gram)
    solved = jax.scipy.linalg.solve_triangular(lower_factor, rounded.T, lower=True)
    return solved.T.astype(jnp.bfloat16)

def split_product(weight_one, right_side):
    quarter = FF // N_TOKEN
    running = jnp.zeros((D, R), jnp.float32)
    for block in range(N_TOKEN):
        product_part = jnp.dot(weight_one[:, block * quarter:(block + 1) * quarter].astype(jnp.float32), right_side[block * quarter:(block + 1) * quarter].astype(jnp.float32), preferred_element_type=jnp.float32)
        running = running + lax.optimization_barrier(product_part.astype(jnp.bfloat16)).astype(jnp.float32)
    return running

def reference(tokens, routes, assign, gate_weight, up_weight, sketch):

    def first_term(bundle):
        return split_product(bundle[0], bundle[1])
    terms = lax.map(first_term, (up_weight, sketch))
    basis = lax.map(orthonormal, jax.ops.segment_sum(terms, assign, num_segments=CLUSTERS))
    for iteration in range(ITERS):

        def gram_term(bundle):
            weight_one, cluster = bundle
            projected = lax.dot_general(weight_one.astype(jnp.float32), basis[cluster].astype(jnp.float32), (((0,), (0,)), ((), ())), preferred_element_type=jnp.float32).astype(jnp.bfloat16)
            return split_product(weight_one, projected)
        terms = lax.map(gram_term, (up_weight, assign))
        basis = lax.map(orthonormal, jax.ops.segment_sum(terms, assign, num_segments=CLUSTERS))
    blocks = EXPERTS * N_TOKEN
    entries = TOK_DEV * TOP
    block_ids = routes.reshape(blocks, entries)
    expert_hits = (block_ids[:, :, None] == jnp.arange(EXPERTS, dtype=jnp.int32)[None, None, :]).astype(jnp.int32)
    earlier = jnp.cumsum(expert_hits, axis=1) - expert_hits
    slot_index = jnp.sum(earlier * expert_hits, axis=2).astype(jnp.int32)
    block_index = jnp.arange(blocks, dtype=jnp.int32)[:, None]
    source_expert = block_index // N_TOKEN
    source_token = block_index % N_TOKEN
    position = ((source_token * EXPERTS + source_expert) * CAP + slot_index).astype(jnp.int32)
    token_index = (block_index * TOK_DEV + jnp.arange(entries, dtype=jnp.int32)[None, :] // TOP).astype(jnp.int32)
    slots_in = jnp.zeros((EXPERTS, SLOTS, D), jnp.bfloat16).at[block_ids, position].set(tokens[token_index])

    def expert_hidden(bundle):
        slot_rows, gate_one, up_one, cluster = bundle
        shared = basis[cluster]
        on_basis = jnp.dot(slot_rows.astype(jnp.float32), shared.astype(jnp.float32), preferred_element_type=jnp.float32).astype(jnp.bfloat16)
        coefficient = lax.dot_general(shared.astype(jnp.float32), up_one.astype(jnp.float32), (((0,), (0,)), ((), ())), preferred_element_type=jnp.float32).astype(jnp.bfloat16)
        gate_value = jnp.dot(slot_rows.astype(jnp.float32), gate_one.astype(jnp.float32), preferred_element_type=jnp.float32)
        merged = jnp.dot(on_basis.astype(jnp.float32), coefficient.astype(jnp.float32), preferred_element_type=jnp.float32)
        return (jax.nn.silu(gate_value) * merged).astype(jnp.bfloat16)
    return lax.map(expert_hidden, (slots_in, gate_weight, up_weight, assign))
```

```python
import jax
import jax.numpy as jnp
from jax import lax
from jax.experimental import pallas as pl
from jax.experimental.pallas import tpu as pltpu
from jax.sharding import PartitionSpec as P

BLK = 128
FULL = lax.Precision.HIGHEST


def leaf_inverse(block):
    lanes = lax.broadcasted_iota(jnp.int32, (8, BLK), 1)
    subs = lax.broadcasted_iota(jnp.int32, (8, BLK), 0)
    groups = BLK // 8
    rows = [block[8 * g:8 * g + 8, :] for g in range(groups)]
    wide = lambda v: jnp.broadcast_to(v, (8, BLK))
    for j in range(0, BLK, 2):
        g, s = j // 8, j % 8
        pair = (lanes == j) | (lanes == j + 1)
        cols = [(wide(rows[i][:, j:j + 1]), wide(rows[i][:, j + 1:j + 2])) for i in range(g, groups)]
        a = wide(cols[0][0][s:s + 1, :])
        b = wide(cols[0][1][s:s + 1, :])
        c = wide(cols[0][1][s + 1:s + 2, :])
        scale = 1.0 / (a * c - b * b)
        first = wide(rows[g][s:s + 1, :])
        second = wide(rows[g][s + 1:s + 2, :])
        first = jnp.where(pair, jnp.where(lanes == j, 1.0, 0.0), first)
        second = jnp.where(pair, jnp.where(lanes == j, 0.0, 1.0), second)
        u1 = (c * first - b * second) * scale
        u2 = (a * second - b * first) * scale
        for i in range(g, groups):
            c1, c2 = cols[i - g]
            if i == g:
                if s == 6:
                    continue
                below = subs > s + 1
                new = jnp.where(pair, 0.0, rows[i]) - c1 * u1 - c2 * u2
                rows[i] = jnp.where(below, new, rows[i])
            else:
                rows[i] = jnp.where(pair, 0.0, rows[i]) - c1 * u1 - c2 * u2
    out = []
    odd = (subs % 2) == 1
    for g in range(groups):
        row_id = subs + 8 * g
        mate = row_id + 1 - 2 * (subs % 2)
        v = rows[g]
        d = wide(jnp.sum(jnp.where(lanes == row_id, v, 0.0), axis=1, keepdims=True))
        o = wide(jnp.sum(jnp.where(lanes == mate, v, 0.0), axis=1, keepdims=True))
        clean = jnp.where(lanes < row_id - (subs % 2), v, 0.0) + jnp.where(lanes == row_id, 1.0, 0.0)
        prev = pltpu.roll(clean, 1, 0)
        d_prev = pltpu.roll(d, 1, 0)
        ratio = jnp.where(odd, o / d_prev, 0.0)
        pivot = jnp.where(odd, d - o * ratio, d)
        out.append((clean - ratio * prev) * lax.rsqrt(pivot))
    return jnp.concatenate(out, axis=0)

def inverse_factor_kernel(gram_ref, out_ref, work_ref):
    n = gram_ref.shape[0]
    work_ref[...] = gram_ref[...]
    row_blk = lax.broadcasted_iota(jnp.int32, (n, n), 0) // BLK
    col_blk = lax.broadcasted_iota(jnp.int32, (n, n), 1) // BLK

    def step(k, carry):
        at = pl.multiple_of(k * BLK, BLK)
        top = leaf_inverse(work_ref[pl.ds(at, BLK), pl.ds(at, BLK)])
        eye = (lax.broadcasted_iota(jnp.int32, (BLK, BLK), 0) == lax.broadcasted_iota(jnp.int32, (BLK, BLK), 1)).astype(jnp.float32)
        work_ref[pl.ds(at, BLK), pl.ds(at, BLK)] = eye
        head = jnp.dot(top, work_ref[pl.ds(at, BLK), :], precision=FULL, preferred_element_type=jnp.float32)
        update = lax.dot_general(head, head, (((0,), (0,)), ((), ())), precision=FULL, preferred_element_type=jnp.float32)
        old = work_ref[...]
        kept = jnp.where(col_blk == k, 0.0, old)
        work_ref[...] = jnp.where(row_blk > k, kept - update, old)
        work_ref[pl.ds(at, BLK), :] = head
        return carry

    lax.fori_loop(0, n // BLK, step, 0)
    out_ref[...] = jnp.where(row_blk >= col_blk, work_ref[...], 0.0)

def inverse_factor(gram):
    n = gram.shape[0]
    return pl.pallas_call(inverse_factor_kernel, out_shape=jax.ShapeDtypeStruct((n, n), jnp.float32),
        scratch_shapes=[pltpu.VMEM((n, n), jnp.float32)], name="inverse_factor")(gram)


def place_tokens(tok_rows, tok_ids, expert_count, capacity):
    flat_ids = tok_ids.reshape(-1)
    expert_hits = (flat_ids[:, None] == jnp.arange(expert_count, dtype=jnp.int32)[None, :]).astype(
        jnp.int32
    )
    earlier = jnp.cumsum(expert_hits, axis=0) - expert_hits
    slot_index = jnp.sum(earlier * expert_hits, axis=1)
    target = flat_ids * capacity + slot_index
    select = (
        jnp.arange(expert_count * capacity, dtype=jnp.int32)[:, None] == target[None, :]
    ).astype(jnp.float32)
    select = (
        select.reshape(expert_count * capacity, tok_rows.shape[0], tok_ids.shape[1])
        .sum(axis=2)
        .astype(jnp.bfloat16)
    )
    filled = jnp.dot(select, tok_rows, preferred_element_type=jnp.float32).astype(jnp.bfloat16)
    return filled.reshape(expert_count, capacity, tok_rows.shape[1])


def exchanged_slots(tokens, routes, expert_count, token_count, capacity):
    shard_rows = tokens.shape[0]
    all_tokens, all_routes = (
        lax.all_gather(tokens, "token", axis=0, tiled=True),
        lax.all_gather(routes, "token", axis=0, tiled=True),
    )

    def place_shard(shard_tokens, shard_routes):
        return place_tokens(shard_tokens, shard_routes, expert_count, capacity)

    stacked = jax.vmap(place_shard)(
        all_tokens.reshape(token_count, shard_rows, tokens.shape[1]),
        all_routes.reshape(token_count, shard_rows, routes.shape[1]),
    )
    slots_in = lax.all_to_all(stacked, "expert", split_axis=1, concat_axis=1, tiled=True)
    return slots_in.reshape(-1, tokens.shape[1])


def gathered_slots(tokens, routes, expert_count, token_count, capacity):
    shard_rows, width = tokens.shape
    top = routes.shape[1]
    own_expert = lax.axis_index("expert")
    own_token = lax.axis_index("token")
    places = jnp.stack([own_expert, own_token]).astype(jnp.int32)
    tail = jnp.concatenate(
        [routes, jnp.broadcast_to(places[None, :], (shard_rows, 2))], axis=1
    ).astype(jnp.bfloat16)
    tail = jnp.pad(tail, ((0, 0), (0, BLK - top - 2)))
    held = jnp.concatenate([tokens, tail], axis=1)

    def spread(held, axis, stride, size):
        count = lax.axis_size(axis)
        pieces = [held]
        for shift in range(1, size):
            moves = []
            for place in range(count):
                digit = place // stride % size
                moves.append((place, place + ((digit + shift) % size - digit) * stride))
            pieces.append(lax.ppermute(held, axis, moves))
        return jnp.concatenate(pieces, axis=0)

    outer = expert_count // (2 * token_count)
    held = spread(held, "expert", 2 * token_count, outer)
    held = spread(held, "expert", 2, token_count)
    held = spread(held, "token", 1, token_count)
    held = spread(held, "expert", 1, 2)
    blocks = expert_count * token_count
    info = held[:, width:].astype(jnp.int32)
    hit = jnp.any(info[:, :top] == own_expert, axis=1)
    by_block = hit.astype(jnp.bfloat16).reshape(blocks, shard_rows)
    before = (
        jnp.arange(shard_rows)[:, None] < jnp.arange(shard_rows)[None, :]
    ).astype(jnp.bfloat16)
    slot = jnp.dot(by_block, before, preferred_element_type=jnp.float32).astype(jnp.int32)
    base = (info[:, top + 1] * expert_count + info[:, top]) * capacity
    target = jnp.where(hit, base + slot.reshape(-1), -1)
    select = (
        jnp.arange(blocks * capacity, dtype=jnp.int32)[:, None] == target[None, :]
    ).astype(jnp.bfloat16)
    return jnp.dot(select, held[:, :width], preferred_element_type=jnp.float32).astype(
        jnp.bfloat16
    )


def shifted(token_count, shift):
    return [(place, (place + shift) % token_count) for place in range(token_count)]


def cluster_rows(weight_blocks, right, same):
    token_count = len(weight_blocks)
    expert_count = same.shape[0]
    parts = []
    for shift in range(1, token_count):
        part = jnp.dot(weight_blocks[shift], right, preferred_element_type=jnp.float32)
        parts.append(
            lax.ppermute(part.astype(jnp.bfloat16), "token", shifted(token_count, shift))
        )
    total = jnp.dot(weight_blocks[0], right, preferred_element_type=jnp.float32)
    total = total.astype(jnp.bfloat16).astype(jnp.float32)
    for part in parts:
        total = total + part.astype(jnp.float32)
    cols = right.shape[1]
    pieces = total.astype(jnp.bfloat16).reshape(expert_count, -1, cols)
    arrived = lax.all_to_all(pieces, "expert", split_axis=0, concat_axis=0, tiled=True)
    outgoing = jnp.einsum("de,erk->drk", same, arrived, preferred_element_type=jnp.float32)
    returned = lax.all_to_all(
        outgoing.astype(jnp.bfloat16), "expert", split_axis=0, concat_axis=0, tiled=True
    )
    own = returned.reshape(-1, cols)
    rows = [own]
    for shift in range(1, token_count):
        rows.append(lax.ppermute(own, "token", shifted(token_count, token_count - shift)))
    return rows


def contract_rows(left, right):
    total = None
    for one, other in zip(left, right):
        part = lax.dot_general(
            one, other, (((0,), (0,)), ((), ())), preferred_element_type=jnp.float32
        )
        total = part if total is None else total + part
    return total


def per_device(tokens, routes, assign, gate_weight, up_weight, sketch):
    expert_count = lax.axis_size("expert")
    token_count = lax.axis_size("token")
    own_token = lax.axis_index("token")
    gate_local = gate_weight[0]
    up_local = up_weight[0]
    features = up_local.shape[0]
    block_rows = features // token_count
    same = (assign[:, None] == assign[None, :]).astype(jnp.bfloat16)

    def row_block(array, shift, axis):
        start = (own_token + shift) % token_count * block_rows
        return lax.dynamic_slice_in_dim(array, start, block_rows, axis)

    blocks = [row_block(up_local, shift, 0) for shift in range(token_count)]
    shard_rows = tokens.shape[0]
    capacity = max(2, 2 * shard_rows * routes.shape[1] // expert_count)
    gathered_bytes = expert_count * token_count * tokens.size * 2
    place = gathered_slots if gathered_bytes <= 1 << 23 else exchanged_slots
    slots_in = place(tokens, routes, expert_count, token_count, capacity)
    gate_value = jnp.dot(slots_in, gate_local, preferred_element_type=jnp.float32)

    first = cluster_rows(blocks, sketch[0], same)
    inverse = inverse_factor(contract_rows(first, first))
    mixed = contract_rows(blocks, first)
    projected = lax.dot_general(
        mixed, inverse, (((1,), (1,)), ((), ())), precision=lax.Precision.HIGH,
        preferred_element_type=jnp.float32,
    ).astype(jnp.bfloat16)
    second = cluster_rows(blocks, projected, same)
    inverse = inverse_factor(contract_rows(second, second))
    mixed = contract_rows(second, blocks)
    slot_mixed = None
    for shift, rows in enumerate(second):
        part = jnp.dot(
            row_block(slots_in, shift, 1), rows, preferred_element_type=jnp.float32
        )
        slot_mixed = part if slot_mixed is None else slot_mixed + part
    coefficient = jnp.dot(
        inverse, mixed, precision=lax.Precision.HIGH, preferred_element_type=jnp.float32
    ).astype(jnp.bfloat16)
    on_basis = lax.dot_general(
        slot_mixed, inverse, (((1,), (1,)), ((), ())), precision=lax.Precision.HIGH,
        preferred_element_type=jnp.float32,
    ).astype(jnp.bfloat16)
    merged = jnp.dot(on_basis, coefficient, preferred_element_type=jnp.float32)
    hidden = (jax.nn.silu(gate_value) * merged).astype(jnp.bfloat16)
    return hidden[None]


def solution(mesh):
    return jax.shard_map(
        per_device,
        mesh=mesh,
        in_specs=(
            P(("expert", "token"), None),
            P(("expert", "token"), None),
            P(),
            P("expert", None, "token"),
            P("expert", None, "token"),
            P("expert", "token", None),
        ),
        out_specs=P("expert", None, "token"),
        check_vma=False,
    )
```

```python
import jax
import jax.numpy as jnp
from jax import lax
from jax.experimental import pallas as pl
from jax.experimental.pallas import tpu as pltpu
from jax.sharding import PartitionSpec as P

BLK = 128
NEAR = 2
FULL = lax.Precision.HIGHEST


def leaf_inverse(block):
    lanes = lax.broadcasted_iota(jnp.int32, (8, BLK), 1)
    subs = lax.broadcasted_iota(jnp.int32, (8, BLK), 0)
    keep = jnp.where(lanes < BLK, 1.0, 0.0)
    groups = BLK // 8
    rows = [block[8 * g:8 * g + 8, :] for g in range(groups)]
    wide = lambda v: jnp.broadcast_to(v, (8, BLK))
    out = []
    for g in range(groups):
        first = 8 * g
        panel = (lanes >= first) & (lanes < first + 8)
        cols = [
            [wide(rows[i][:, first + q:first + q + 1]) for q in range(8)]
            for i in range(g, min(g + 1 + NEAR, groups))
        ]
        pivot_cols = [col * keep for col in cols[0]]
        pivot = [[wide(pivot_cols[q][l:l + 1, :]) for q in range(8)] for l in range(8)]
        lines = [
            jnp.where(panel, jnp.where(lanes == first + l, 1.0, 0.0), wide(rows[g][l:l + 1, :]))
            for l in range(8)
        ]
        ratio = [[None] * 8 for _ in range(8)]
        scaled = []
        done = None
        for k in range(8):
            reciprocal = 1.0 / pivot[k][k]
            for l in range(k + 1, 8):
                ratio[k][l] = pivot[k][l] * reciprocal
                for q in range(l, 8):
                    pivot[l][q] = pivot[l][q] - ratio[k][l] * pivot[k][q]
                lines[l] = lines[l] - ratio[k][l] * lines[k]
            scaled.append(lines[k] * reciprocal)
            final = lines[k] * lax.rsqrt(pivot[k][k])
            done = final if done is None else jnp.where(subs == k, final, done)
        out.append(jnp.where(lanes < first + 8, done, 0.0))
        for k in reversed(range(7)):
            for l in range(k + 1, 8):
                scaled[k] = scaled[k] - ratio[k][l] * scaled[l]
        for i in range(g + 1, min(g + 1 + NEAR, groups)):
            terms = [cols[i - g][q] * scaled[q] for q in range(8)]
            while len(terms) > 1:
                terms = [terms[p] + terms[p + 1] for p in range(0, len(terms), 2)]
            rows[i] = jnp.where(panel, 0.0, rows[i]) - terms[0]
        far = g + 1 + NEAR
        if far < groups:
            left = jnp.concatenate(rows[far:], axis=0)
            inside = (lax.broadcasted_iota(jnp.int32, left.shape, 1) >= first) & (
                lax.broadcasted_iota(jnp.int32, left.shape, 1) < first + 8)
            packed = scaled[0]
            for q in range(1, 8):
                packed = jnp.where(subs == q, scaled[q], packed)
            zero = jnp.zeros((8, BLK), jnp.float32)
            right = jnp.concatenate([packed if i == g else zero for i in range(groups)], axis=0)
            change = jnp.dot(jnp.where(inside, left, 0.0), right, precision=FULL, preferred_element_type=jnp.float32)
            left = jnp.where(inside, 0.0, left) - change
            for i in range(far, groups):
                rows[i] = left[8 * (i - far):8 * (i - far) + 8, :]
    return jnp.concatenate(out, axis=0)

def inverse_factor_kernel(gram_ref, out_ref, work_ref):
    n = gram_ref.shape[0]
    work_ref[...] = gram_ref[...]
    row_blk = lax.broadcasted_iota(jnp.int32, (n, n), 0) // BLK
    col_blk = lax.broadcasted_iota(jnp.int32, (n, n), 1) // BLK

    def step(k, carry):
        at = pl.multiple_of(k * BLK, BLK)
        top = leaf_inverse(work_ref[pl.ds(at, BLK), pl.ds(at, BLK)])
        eye = (lax.broadcasted_iota(jnp.int32, (BLK, BLK), 0) == lax.broadcasted_iota(jnp.int32, (BLK, BLK), 1)).astype(jnp.float32)
        work_ref[pl.ds(at, BLK), pl.ds(at, BLK)] = eye
        head = jnp.dot(top, work_ref[pl.ds(at, BLK), :], precision=FULL, preferred_element_type=jnp.float32)
        update = lax.dot_general(head, head, (((0,), (0,)), ((), ())), precision=FULL, preferred_element_type=jnp.float32)
        old = work_ref[...]
        kept = jnp.where(col_blk == k, 0.0, old)
        work_ref[...] = jnp.where(row_blk > k, kept - update, old)
        work_ref[pl.ds(at, BLK), :] = head
        return carry

    lax.fori_loop(0, n // BLK, step, 0)
    out_ref[...] = jnp.where(row_blk >= col_blk, work_ref[...], 0.0)

def inverse_factor(gram):
    n = gram.shape[0]
    return pl.pallas_call(inverse_factor_kernel, out_shape=jax.ShapeDtypeStruct((n, n), jnp.float32),
        scratch_shapes=[pltpu.VMEM((n, n), jnp.float32)], name="inverse_factor")(gram)


def place_tokens(tok_rows, tok_ids, expert_count, capacity):
    flat_ids = tok_ids.reshape(-1)
    expert_hits = (flat_ids[:, None] == jnp.arange(expert_count, dtype=jnp.int32)[None, :]).astype(
        jnp.int32
    )
    earlier = jnp.cumsum(expert_hits, axis=0) - expert_hits
    slot_index = jnp.sum(earlier * expert_hits, axis=1)
    target = flat_ids * capacity + slot_index
    select = (
        jnp.arange(expert_count * capacity, dtype=jnp.int32)[:, None] == target[None, :]
    ).astype(jnp.float32)
    select = (
        select.reshape(expert_count * capacity, tok_rows.shape[0], tok_ids.shape[1])
        .sum(axis=2)
        .astype(jnp.bfloat16)
    )
    filled = jnp.dot(select, tok_rows, preferred_element_type=jnp.float32).astype(jnp.bfloat16)
    return filled.reshape(expert_count, capacity, tok_rows.shape[1])


def exchanged_slots(tokens, routes, expert_count, token_count, capacity):
    shard_rows = tokens.shape[0]
    all_tokens, all_routes = (
        lax.all_gather(tokens, "token", axis=0, tiled=True),
        lax.all_gather(routes, "token", axis=0, tiled=True),
    )

    def place_shard(shard_tokens, shard_routes):
        return place_tokens(shard_tokens, shard_routes, expert_count, capacity)

    stacked = jax.vmap(place_shard)(
        all_tokens.reshape(token_count, shard_rows, tokens.shape[1]),
        all_routes.reshape(token_count, shard_rows, routes.shape[1]),
    )
    slots_in = lax.all_to_all(stacked, "expert", split_axis=1, concat_axis=1, tiled=True)
    return slots_in.reshape(-1, tokens.shape[1])


def gathered_slots(tokens, routes, expert_count, token_count, capacity):
    shard_rows, width = tokens.shape
    top = routes.shape[1]
    own_expert = lax.axis_index("expert")
    own_token = lax.axis_index("token")
    places = jnp.stack([own_expert, own_token]).astype(jnp.int32)
    tail = jnp.concatenate(
        [routes, jnp.broadcast_to(places[None, :], (shard_rows, 2))], axis=1
    ).astype(jnp.bfloat16)
    tail = jnp.pad(tail, ((0, 0), (0, BLK - top - 2)))
    held = jnp.concatenate([tokens, tail], axis=1)

    def spread(held, axis, stride, size):
        count = lax.axis_size(axis)
        pieces = [held]
        for shift in range(1, size):
            moves = []
            for place in range(count):
                digit = place // stride % size
                moves.append((place, place + ((digit + shift) % size - digit) * stride))
            pieces.append(lax.ppermute(held, axis, moves))
        return jnp.concatenate(pieces, axis=0)

    outer = expert_count // (2 * token_count)
    held = spread(held, "expert", 2 * token_count, outer)
    held = spread(held, "expert", 2, token_count)
    held = spread(held, "token", 1, token_count)
    held = spread(held, "expert", 1, 2)
    blocks = expert_count * token_count
    info = held[:, width:].astype(jnp.int32)
    hit = jnp.any(info[:, :top] == own_expert, axis=1)
    by_block = hit.astype(jnp.bfloat16).reshape(blocks, shard_rows)
    before = (
        jnp.arange(shard_rows)[:, None] < jnp.arange(shard_rows)[None, :]
    ).astype(jnp.bfloat16)
    slot = jnp.dot(by_block, before, preferred_element_type=jnp.float32).astype(jnp.int32)
    base = (info[:, top + 1] * expert_count + info[:, top]) * capacity
    target = jnp.where(hit, base + slot.reshape(-1), -1)
    select = (
        jnp.arange(blocks * capacity, dtype=jnp.int32)[:, None] == target[None, :]
    ).astype(jnp.bfloat16)
    return jnp.dot(select, held[:, :width], preferred_element_type=jnp.float32).astype(
        jnp.bfloat16
    )


def shifted(token_count, shift):
    return [(place, (place + shift) % token_count) for place in range(token_count)]


def cluster_rows(weight_blocks, right, same):
    token_count = len(weight_blocks)
    expert_count = same.shape[0]
    parts = []
    for shift in range(1, token_count):
        part = jnp.dot(weight_blocks[shift], right, preferred_element_type=jnp.float32)
        parts.append(
            lax.ppermute(part.astype(jnp.bfloat16), "token", shifted(token_count, shift))
        )
    total = jnp.dot(weight_blocks[0], right, preferred_element_type=jnp.float32)
    total = total.astype(jnp.bfloat16).astype(jnp.float32)
    for part in parts:
        total = total + part.astype(jnp.float32)
    cols = right.shape[1]
    pieces = total.astype(jnp.bfloat16).reshape(expert_count, -1, cols)
    arrived = lax.all_to_all(pieces, "expert", split_axis=0, concat_axis=0, tiled=True)
    outgoing = jnp.einsum("de,erk->drk", same, arrived, preferred_element_type=jnp.float32)
    returned = lax.all_to_all(
        outgoing.astype(jnp.bfloat16), "expert", split_axis=0, concat_axis=0, tiled=True
    )
    own = returned.reshape(-1, cols)
    rows = [own]
    for shift in range(1, token_count):
        rows.append(lax.ppermute(own, "token", shifted(token_count, token_count - shift)))
    return rows


def contract_rows(left, right):
    total = None
    for one, other in zip(left, right):
        part = lax.dot_general(
            one, other, (((0,), (0,)), ((), ())), preferred_element_type=jnp.float32
        )
        total = part if total is None else total + part
    return total


def per_device(tokens, routes, assign, gate_weight, up_weight, sketch):
    expert_count = lax.axis_size("expert")
    token_count = lax.axis_size("token")
    own_token = lax.axis_index("token")
    gate_local = gate_weight[0]
    up_local = up_weight[0]
    features = up_local.shape[0]
    block_rows = features // token_count
    same = (assign[:, None] == assign[None, :]).astype(jnp.bfloat16)

    def row_block(array, shift, axis):
        start = (own_token + shift) % token_count * block_rows
        return lax.dynamic_slice_in_dim(array, start, block_rows, axis)

    blocks = [row_block(up_local, shift, 0) for shift in range(token_count)]
    shard_rows = tokens.shape[0]
    capacity = max(2, 2 * shard_rows * routes.shape[1] // expert_count)
    gathered_bytes = expert_count * token_count * tokens.size * 2
    place = gathered_slots if gathered_bytes <= 1 << 23 else exchanged_slots
    slots_in = place(tokens, routes, expert_count, token_count, capacity)
    gate_value = jnp.dot(slots_in, gate_local, preferred_element_type=jnp.float32)

    first = cluster_rows(blocks, sketch[0], same)
    inverse = inverse_factor(contract_rows(first, first))
    mixed = contract_rows(blocks, first)
    projected = lax.dot_general(
        mixed, inverse, (((1,), (1,)), ((), ())), precision=lax.Precision.HIGH,
        preferred_element_type=jnp.float32,
    ).astype(jnp.bfloat16)
    second = cluster_rows(blocks, projected, same)
    inverse = inverse_factor(contract_rows(second, second))
    mixed = contract_rows(second, blocks)
    slot_mixed = None
    for shift, rows in enumerate(second):
        part = jnp.dot(
            row_block(slots_in, shift, 1), rows, preferred_element_type=jnp.float32
        )
        slot_mixed = part if slot_mixed is None else slot_mixed + part
    coefficient = jnp.dot(
        inverse, mixed, precision=lax.Precision.HIGH, preferred_element_type=jnp.float32
    ).astype(jnp.bfloat16)
    on_basis = lax.dot_general(
        slot_mixed, inverse, (((1,), (1,)), ((), ())), precision=lax.Precision.HIGH,
        preferred_element_type=jnp.float32,
    ).astype(jnp.bfloat16)
    merged = jnp.dot(on_basis, coefficient, preferred_element_type=jnp.float32)
    hidden = (jax.nn.silu(gate_value) * merged).astype(jnp.bfloat16)
    return hidden[None]


def solution(mesh):
    return jax.shard_map(
        per_device,
        mesh=mesh,
        in_specs=(
            P(("expert", "token"), None),
            P(("expert", "token"), None),
            P(),
            P("expert", None, "token"),
            P("expert", None, "token"),
            P("expert", "token", None),
        ),
        out_specs=P("expert", None, "token"),
        check_vma=False,
    )
```
